32 devices in a mesh: chan: 8 (over z, y), seg: 4 (over x, core).
Axes of the slice: x: 2, y: 2, z: 4, core: 2. Of those that a mesh axis runs over, the one named last changes fastest.
Arguments:
- traces: bfloat16 [1024, 8192], P('chan', 'seg'), may hold values from -36 to 36
- pair_bins: int32 [2, 1024, 128], P(None, 'chan'), may hold values from 0 to 255
Outputs:
- correlograms: float32 [65, 256], P(None, 'chan')
The draws below stay inside these ranges and needn't reach their ends.
All inputs are finite; a program needn't handle non-finite values.
Results may differ from the reference program's by a relative error of at most 0.0029.
Values may be sent and summed in bfloat16 or wider, within the bound.
A program may use at most 64 MiB of HBM per device.

```python
import math
import jax
import jax.numpy as jnp
from jax import lax

CB = 128
SEG_LEN = 2048
MAX_LAG = 32
NB = 256
ROUNDS = 2
LAGS = 65
CHANNELS = 1024
TIME = 8192
PAIRS_BIN = 1024
N_CHAN = 8
N_SEG = 4


def draw_traces(key, part):
    key_gain = jax.random.fold_in(key, 11)
    key_noise = jax.random.fold_in(key, 12)
    position = jnp.arange(TIME, dtype=jnp.float32) / (TIME - 1)
    gains = jnp.exp(jax.random.uniform(key_gain, (CHANNELS, 1), jnp.float32, math.log(0.3), math.log(3.0)))
    noise = jax.random.truncated_normal(key_noise, -4.0, 4.0, (CHANNELS, TIME), jnp.float32)
    envelope = 1.0 + 2.0 * position
    return (gains * envelope[None, :] * noise).astype(jnp.bfloat16)


def place_ends(drawn, rng, least, top_value):
    index_at = [jax.random.randint(jax.random.fold_in(rng, axis), (), 0, length) for axis, length in enumerate(drawn.shape)]
    widest = drawn.shape.index(max(drawn.shape))
    neighbour = index_at[:widest] + [(index_at[widest] + 1) % drawn.shape[widest]] + index_at[widest + 1:]
    return drawn.at[tuple(index_at)].set(least).at[tuple(neighbour)].set(top_value)


def setup_inputs(seed: int = 0) -> dict:
    key_list = jax.random.split(jax.random.key(seed), 3)
    traces = draw_traces(jax.random.fold_in(key_list[2], 71), 0)
    pair_bins = place_ends(jax.random.randint(key_list[1], (ROUNDS, CHANNELS, CB), 0, NB), jax.random.fold_in(key_list[1], 1), 0, NB - 1).astype(jnp.int32)
    return dict(traces=traces, pair_bins=pair_bins)


EPSILON = 1e-06

def segment_bins(own_block, partner, own_scale, partner_scale, round_bins):
    padded = jnp.pad(partner.astype(jnp.float32), ((0, 0), (MAX_LAG, MAX_LAG)))
    offsets = jnp.arange(LAGS, dtype=jnp.int32)
    shifted = jax.vmap(lambda offset: lax.dynamic_slice_in_dim(padded, offset, SEG_LEN, 1))(offsets)
    raw_sums = jnp.einsum('at,lbt->alb', own_block.astype(jnp.float32), shifted)
    zscore = raw_sums * own_scale[:, None, None] * partner_scale[None, None, :] * (1.0 / math.sqrt(TIME))
    rounded = lax.optimization_barrier(zscore.astype(jnp.bfloat16)).astype(jnp.float32)
    bin_ids = jnp.arange(NB, dtype=jnp.int32)
    onehot = (round_bins[:, :, None] == bin_ids[None, None, :]).astype(jnp.float32)
    return jnp.einsum('alb,abn->ln', rounded, onehot)

def reference(traces, pair_bins):
    squares = lax.optimization_barrier(jnp.sum(jnp.square(traces.astype(jnp.float32)), axis=1))
    inv_rms = lax.rsqrt(squares / TIME + EPSILON)
    blocks = traces.reshape(N_CHAN, CB, N_SEG, SEG_LEN)
    scales = inv_rms.reshape(N_CHAN, CB)
    bin_blocks = pair_bins.reshape(ROUNDS, N_CHAN, CB, CB)
    total = jnp.zeros((LAGS, NB), jnp.float32)
    for round_index in range(ROUNDS):
        distance = N_CHAN // 2 - round_index

        def step_pair(carry, flat_index):
            block_index = flat_index // N_SEG
            segment = flat_index % N_SEG
            partner_index = (block_index + distance) % N_CHAN
            own_block = blocks[block_index, :, segment, :]
            partner = blocks[partner_index, :, segment, :]
            term = segment_bins(own_block, partner, scales[block_index], scales[partner_index], bin_blocks[round_index, block_index])
            return (carry + term, None)
        total, _ = lax.scan(step_pair, total, jnp.arange(N_CHAN * N_SEG, dtype=jnp.int32))
    return total * (1.0 / math.sqrt(PAIRS_BIN))
```

```python
import functools
import math

import jax
import jax.numpy as jnp
from jax import lax
from jax.experimental import pallas as pl
from jax.experimental.pallas import tpu as pltpu
from jax.sharding import PartitionSpec as P

MAX_LAG = 32
NB = 256
ROUNDS = 2
LAGS = 2 * MAX_LAG + 1
EPSILON = 1e-06

FINE = 8
COARSE = MAX_LAG // FINE
LANES = 128
MESH = pl.DeviceIdType.MESH
CONTRACT = (((1,), (1,)), ((), ()))


def from_behind(block, axis, distance):
    devices = range(lax.axis_size(axis))
    route = [((i - distance) % len(devices), i) for i in devices]
    return lax.ppermute(block, axis, route)


def own_shifts(own):
    channels, length = own.shape
    padded = jnp.pad(own, ((0, 0), (FINE, FINE)))
    sides = []
    for first in (-FINE, 0):
        rows = [lax.slice_in_dim(padded, FINE - s, FINE - s + length, axis=1) for s in range(first, first + FINE)]
        sides.append(jnp.stack(rows, 1).reshape(channels * FINE, length))
    return sides


def partner_shifts(partner):
    length = partner.shape[1]
    padded = jnp.pad(partner, ((0, 0), (MAX_LAG, MAX_LAG)))
    starts = range(FINE, 2 * MAX_LAG + 1, FINE)
    return jnp.concatenate([lax.slice_in_dim(padded, start, start + length, axis=1) for start in starts], 0)


def stack_kernel(group, minus_ref, plus_ref, own_ref, partner_ref, scale_ref, bins_ref, out_ref, neg, pos, last, total):
    channels = own_ref.shape[0]
    width = partner_ref.shape[0] // (2 * COARSE)
    step = pl.program_id(0)

    @pl.when(step == 0)
    def _():
        total[...] = jnp.zeros_like(total)

    def dot(left, right):
        return lax.dot_general(left, right, CONTRACT, preferred_element_type=jnp.float32)

    neg[...] = dot(minus_ref[...], partner_ref[: COARSE * width])
    pos[...] = dot(plus_ref[...], partner_ref[(COARSE - 1) * width : (2 * COARSE - 1) * width])
    last[...] = dot(own_ref[...], partner_ref[(2 * COARSE - 1) * width :])

    bin_ids = lax.broadcasted_iota(jnp.int32, (NB, width), 0)

    @pl.loop(0, channels // group)
    def _(g):
        base = pl.multiple_of(g * group, group)
        scale = scale_ref[pl.ds(base, group), :]
        bins = bins_ref[pl.ds(base, group), :]
        top = last[pl.ds(base, group), :]
        scores, hots = [], []
        for a in range(group):
            rows = pl.ds(pl.multiple_of((base + a) * FINE, FINE), FINE)
            factor = jnp.broadcast_to(scale[a : a + 1], (FINE, width))
            pieces = []
            for side in (neg, pos):
                for k in range(COARSE):
                    pieces.append(side[rows, k * width : (k + 1) * width] * factor)
            edge = jnp.broadcast_to(top[a : a + 1], (FINE, width)) * factor
            pieces += [edge, edge]
            scores.append(jnp.concatenate(pieces, 0).astype(jnp.bfloat16))
            hit = jnp.broadcast_to(bins[a : a + 1], (NB, width)) == bin_ids
            hots.append(jnp.where(hit, 1.0, 0.0).astype(jnp.bfloat16))
        total[...] += dot(jnp.concatenate(scores, 1), jnp.concatenate(hots, 1))

    @pl.when(step == pl.num_programs(0) - 1)
    def _():
        out_ref[...] = total[...]


def round_stack(minus, plus, own, shifted, scale, bins):
    channels, length = own.shape
    step = channels // 2
    lag_rows = 2 * MAX_LAG + 2 * FINE
    fixed = lambda i: (0, 0)
    moving = lambda i: (i, 0)
    return pl.pallas_call(
        functools.partial(stack_kernel, 8),
        out_shape=jax.ShapeDtypeStruct((lag_rows, NB), jnp.float32),
        grid=(channels // step,),
        in_specs=[
            pl.BlockSpec((step * FINE, length), moving),
            pl.BlockSpec((step * FINE, length), moving),
            pl.BlockSpec((step, length), moving),
            pl.BlockSpec(shifted.shape, fixed),
            pl.BlockSpec((step, channels), moving),
            pl.BlockSpec((step, channels), moving),
        ],
        out_specs=pl.BlockSpec((lag_rows, NB), fixed),
        scratch_shapes=[
            pltpu.VMEM((step * FINE, COARSE * channels), jnp.float32),
            pltpu.VMEM((step * FINE, COARSE * channels), jnp.float32),
            pltpu.VMEM((step, channels), jnp.float32),
            pltpu.VMEM((lag_rows, NB), jnp.float32),
        ],
        compiler_params=pltpu.CompilerParams(vmem_limit_bytes=48 * 1024 * 1024),
        cost_estimate=pl.CostEstimate(
            flops=2 * LAGS * channels * channels * length,
            bytes_accessed=4 * channels * FINE * length * 2,
            transcendentals=0,
        ),
    )(minus, plus, own, shifted, scale, bins)


def reduce_kernel(n_chan, n_seg, part_ref, out_ref, arrived, mine, others, send1, recv1, send2, recv2):
    chan, seg = lax.axis_index("chan"), lax.axis_index("seg")
    rows = out_ref.shape[0]
    chan_peers = [lax.rem(chan + k, n_chan) for k in range(1, n_chan)]
    seg_peers = [lax.rem(seg + k, n_seg) for k in range(1, n_seg)]
    barrier = pltpu.get_barrier_semaphore()
    for peer in chan_peers:
        pl.semaphore_signal(barrier, inc=1, device_id=(peer, seg), device_id_type=MESH)
    for peer in seg_peers:
        pl.semaphore_signal(barrier, inc=1, device_id=(chan, peer), device_id_type=MESH)
    pl.semaphore_wait(barrier, n_chan + n_seg - 2)

    first = []
    for k, peer in enumerate(chan_peers):
        copy = pltpu.make_async_remote_copy(
            src_ref=part_ref.at[pl.ds(pl.multiple_of(peer * rows, rows), rows)],
            dst_ref=arrived.at[k],
            send_sem=send1.at[k],
            recv_sem=recv1.at[k],
            device_id=(peer, seg),
            device_id_type=MESH,
        )
        copy.start()
        first.append(copy)
    running = part_ref[pl.ds(pl.multiple_of(chan * rows, rows), rows), :]
    for k, copy in enumerate(first):
        copy.wait()
        running = running + arrived[k]
    mine[...] = running
    second = []
    for k, peer in enumerate(seg_peers):
        copy = pltpu.make_async_remote_copy(
            src_ref=mine,
            dst_ref=others.at[k],
            send_sem=send2.at[k],
            recv_sem=recv2.at[k],
            device_id=(chan, peer),
            device_id_type=MESH,
        )
        copy.start()
        second.append(copy)
    for copy in second:
        copy.wait()
    for position in range(n_seg):
        slot = lax.rem(seg - position + n_seg - 1 + n_seg, n_seg)
        term = jnp.where(slot == n_seg - 1, running, others[jnp.minimum(slot, n_seg - 2)])
        sums = term if position == 0 else sums + term
    out_ref[...] = sums


def reduce_all(part):
    n_chan, n_seg = lax.axis_size("chan"), lax.axis_size("seg")
    rows = part.shape[0] // n_chan
    block = (rows, part.shape[1])
    return pl.pallas_call(
        functools.partial(reduce_kernel, n_chan, n_seg),
        out_shape=jax.ShapeDtypeStruct(block, jnp.float32),
        in_specs=[pl.BlockSpec(memory_space=pltpu.VMEM)],
        out_specs=pl.BlockSpec(memory_space=pltpu.VMEM),
        scratch_shapes=[
            pltpu.VMEM((n_chan - 1,) + block, jnp.float32),
            pltpu.VMEM(block, jnp.float32),
            pltpu.VMEM((n_seg - 1,) + block, jnp.float32),
            pltpu.SemaphoreType.DMA((n_chan - 1,)),
            pltpu.SemaphoreType.DMA((n_chan - 1,)),
            pltpu.SemaphoreType.DMA((n_seg - 1,)),
            pltpu.SemaphoreType.DMA((n_seg - 1,)),
        ],
        compiler_params=pltpu.CompilerParams(
            collective_id=0, has_side_effects=True, vmem_limit_bytes=16 * 1024 * 1024
        ),
    )(part)


def local(traces, pair_bins):
    channels, seg_length = traces.shape
    chan_count = lax.axis_size("chan")
    seg_count = lax.axis_size("seg")
    total_time = seg_length * seg_count
    time_scale = 1.0 / math.sqrt(total_time)
    half_loop = chan_count // 2
    far_block = from_behind(traces, "chan", -half_loop)
    near_block = from_behind(traces, "chan", 1 - half_loop)
    energy = lax.psum(jnp.sum(jnp.square(traces.astype(jnp.float32)), axis=1), "seg")
    scale = lax.rsqrt(energy / total_time + EPSILON)
    far_scale = from_behind(scale, "chan", -half_loop)
    near_scale = from_behind(scale, "chan", 1 - half_loop)
    minus, plus = own_shifts(traces)

    def partial_stack(block, block_scale, bins):
        pair_scale = scale[:, None] * block_scale[None, :] * time_scale
        return round_stack(minus, plus, traces, partner_shifts(block), pair_scale, bins)

    part = partial_stack(far_block, far_scale, pair_bins[0])
    part = part + partial_stack(near_block, near_scale, pair_bins[1])
    pair_total = ROUNDS * chan_count * channels * channels // NB
    part = part.T * (1.0 / math.sqrt(pair_total))
    part = jnp.pad(part, ((0, 0), (0, -part.shape[1] % LANES)))
    return reduce_all(part).T[:LAGS]


def solution(mesh):
    in_specs = (P("chan", "seg"), P(None, "chan", None))
    out_specs = P(None, "chan")
    return jax.shard_map(local, mesh=mesh, in_specs=in_specs, out_specs=out_specs, check_vma=False)
```

```python
import functools
import math

import jax
import jax.numpy as jnp
from jax import lax
from jax.experimental import pallas as pl
from jax.experimental.pallas import tpu as pltpu
from jax.sharding import PartitionSpec as P

MAX_LAG = 32
NB = 256
ROUNDS = 2
LAGS = 2 * MAX_LAG + 1
EPSILON = 1e-06

FINE = 8
COARSE = MAX_LAG // FINE
LANES = 128
CHUNKS = 4
MESH = pl.DeviceIdType.MESH
CONTRACT = (((1,), (1,)), ((), ()))


def from_behind(block, axis, distance):
    devices = range(lax.axis_size(axis))
    route = [((i - distance) % len(devices), i) for i in devices]
    return lax.ppermute(block, axis, route)


def coarse_shifts(block):
    length = block.shape[1]
    padded = jnp.pad(block, ((0, 0), (MAX_LAG, MAX_LAG)))
    starts = range(FINE, 2 * MAX_LAG + 1, FINE)
    return jnp.concatenate([lax.slice_in_dim(padded, start, start + length, axis=1) for start in starts], 0)


def stack_kernel(group, first, far_ref, near_ref, scale_ref, bins_ref, prior_ref, out_ref, fine, neg, pos, last):
    channels, length = far_ref.shape
    width = near_ref.shape[0] // (2 * COARSE)

    def dot(left, right):
        return lax.dot_general(left, right, CONTRACT, preferred_element_type=jnp.float32)

    pair = 2
    tile = pair * FINE
    blank = jnp.zeros((FINE, LANES), jnp.float32)
    for block in range(channels // tile):
        wide = far_ref[block * tile : (block + 1) * tile, :].astype(jnp.float32)
        for start in range(0, tile, pair):
            both = []
            for x in range(start, start + pair):
                row = jnp.broadcast_to(wide[x : x + 1], (FINE, length))
                both.append(jnp.concatenate([row, blank], 1))
            rows = slice((block * tile + start) * FINE, (block * tile + start + pair) * FINE)
            for side, base in ((0, LANES + length - FINE), (1, 0)):
                turned = [pltpu.roll(row, base, 1, stride=1, stride_axis=0)[:, :length] for row in both]
                fine[side, rows, :] = jnp.concatenate(turned, 0).astype(jnp.bfloat16)

    neg[...] = dot(fine[0], near_ref[: COARSE * width])
    pos[...] = dot(fine[1], near_ref[(COARSE - 1) * width : (2 * COARSE - 1) * width])
    last[...] = dot(far_ref[...], near_ref[(2 * COARSE - 1) * width :])

    bin_ids = lax.broadcasted_iota(jnp.int32, (NB, width), 0)
    out_ref[...] = jnp.zeros_like(out_ref) if first else prior_ref[...]

    @pl.loop(0, channels // group)
    def _(g):
        base = pl.multiple_of(g * group, group)
        scale = scale_ref[pl.ds(base, group), :]
        bins = bins_ref[pl.ds(base, group), :]
        top = last[pl.ds(base, group), :]
        for half in range(0, group, group // 2):
            scores, hots = [], []
            for x in range(half, half + group // 2):
                rows = pl.ds(pl.multiple_of((base + x) * FINE, FINE), FINE)
                factor = jnp.broadcast_to(scale[x : x + 1], (FINE, width))
                pieces = []
                for side in (neg, pos):
                    for k in range(COARSE):
                        pieces.append(side[rows, k * width : (k + 1) * width] * factor)
                edge = jnp.broadcast_to(top[x : x + 1], (FINE, width)) * factor
                pieces += [edge, edge]
                scores.append(jnp.concatenate(pieces, 0).astype(jnp.bfloat16))
                hit = jnp.broadcast_to(bins[x : x + 1], (NB, width)) == bin_ids
                hots.append(jnp.where(hit, 1.0, 0.0).astype(jnp.bfloat16))
            out_ref[...] += dot(jnp.concatenate(scores, 1), jnp.concatenate(hots, 1))


def chunk_stack(far, near, scale, bins, prior):
    channels, length = far.shape
    width = near.shape[0] // (2 * COARSE)
    lag_rows = 2 * MAX_LAG + 2 * FINE
    first = prior is None
    if first:
        prior = jnp.zeros((8, LANES), jnp.float32)
    return pl.pallas_call(
        functools.partial(stack_kernel, 8, first),
        out_shape=jax.ShapeDtypeStruct((lag_rows, NB), jnp.float32),
        in_specs=[pl.BlockSpec(memory_space=pltpu.VMEM)] * 5,
        out_specs=pl.BlockSpec(memory_space=pltpu.VMEM),
        scratch_shapes=[
            pltpu.VMEM((2, channels * FINE, length), jnp.bfloat16),
            pltpu.VMEM((channels * FINE, COARSE * width), jnp.float32),
            pltpu.VMEM((channels * FINE, COARSE * width), jnp.float32),
            pltpu.VMEM((channels, width), jnp.float32),
        ],
        compiler_params=pltpu.CompilerParams(vmem_limit_bytes=32 * 1024 * 1024),
        cost_estimate=pl.CostEstimate(
            flops=2 * LAGS * channels * width * length, bytes_accessed=near.size * 2, transcendentals=0
        ),
    )(far, near, scale, bins, prior)


def reduce_kernel(n_chan, n_seg, part_ref, out_ref, arrived, mine, others, send1, recv1, send2, recv2):
    chan, seg = lax.axis_index("chan"), lax.axis_index("seg")
    rows = out_ref.shape[0]
    chan_peers = [lax.rem(chan + k, n_chan) for k in range(1, n_chan)]
    seg_peers = [lax.rem(seg + k, n_seg) for k in range(1, n_seg)]
    barrier = pltpu.get_barrier_semaphore()
    for peer in chan_peers:
        pl.semaphore_signal(barrier, inc=1, device_id=(peer, seg), device_id_type=MESH)
    for peer in seg_peers:
        pl.semaphore_signal(barrier, inc=1, device_id=(chan, peer), device_id_type=MESH)
    pl.semaphore_wait(barrier, n_chan + n_seg - 2)

    first = []
    for k, peer in enumerate(chan_peers):
        copy = pltpu.make_async_remote_copy(
            src_ref=part_ref.at[pl.ds(pl.multiple_of(peer * rows, rows), rows)],
            dst_ref=arrived.at[k],
            send_sem=send1.at[k],
            recv_sem=recv1.at[k],
            device_id=(peer, seg),
            device_id_type=MESH,
        )
        copy.start()
        first.append(copy)
    running = part_ref[pl.ds(pl.multiple_of(chan * rows, rows), rows), :]
    for k, copy in enumerate(first):
        copy.wait()
        running = running + arrived[k]
    mine[...] = running
    second = []
    for k, peer in enumerate(seg_peers):
        copy = pltpu.make_async_remote_copy(
            src_ref=mine,
            dst_ref=others.at[k],
            send_sem=send2.at[k],
            recv_sem=recv2.at[k],
            device_id=(chan, peer),
            device_id_type=MESH,
        )
        copy.start()
        second.append(copy)
    for copy in second:
        copy.wait()
    for position in range(n_seg):
        slot = lax.rem(seg - position + n_seg - 1 + n_seg, n_seg)
        term = jnp.where(slot == n_seg - 1, running, others[jnp.minimum(slot, n_seg - 2)])
        sums = term if position == 0 else sums + term
    out_ref[...] = sums


def reduce_all(part):
    n_chan, n_seg = lax.axis_size("chan"), lax.axis_size("seg")
    rows = part.shape[0] // n_chan
    block = (rows, part.shape[1])
    return pl.pallas_call(
        functools.partial(reduce_kernel, n_chan, n_seg),
        out_shape=jax.ShapeDtypeStruct(block, jnp.float32),
        in_specs=[pl.BlockSpec(memory_space=pltpu.VMEM)],
        out_specs=pl.BlockSpec(memory_space=pltpu.VMEM),
        scratch_shapes=[
            pltpu.VMEM((n_chan - 1,) + block, jnp.float32),
            pltpu.VMEM(block, jnp.float32),
            pltpu.VMEM((n_seg - 1,) + block, jnp.float32),
            pltpu.SemaphoreType.DMA((n_chan - 1,)),
            pltpu.SemaphoreType.DMA((n_chan - 1,)),
            pltpu.SemaphoreType.DMA((n_seg - 1,)),
            pltpu.SemaphoreType.DMA((n_seg - 1,)),
        ],
        compiler_params=pltpu.CompilerParams(
            collective_id=0, has_side_effects=True, vmem_limit_bytes=16 * 1024 * 1024
        ),
    )(part)


def local(traces, pair_bins):
    channels, seg_length = traces.shape
    chan_count = lax.axis_size("chan")
    seg_count = lax.axis_size("seg")
    total_time = seg_length * seg_count
    time_scale = 1.0 / math.sqrt(total_time)
    half_loop = chan_count // 2
    next_block = from_behind(traces, "chan", -1)
    next_bins = from_behind(pair_bins[1], "chan", -1)
    size = channels // CHUNKS
    far_chunks = [from_behind(traces[k * size : (k + 1) * size], "chan", -half_loop) for k in range(CHUNKS)]
    energy = lax.psum(jnp.sum(jnp.square(traces.astype(jnp.float32)), axis=1), "seg")
    scale = lax.rsqrt(energy / total_time + EPSILON)
    far_scale = from_behind(scale, "chan", -half_loop)
    next_scale = from_behind(scale, "chan", -1)
    near = coarse_shifts(jnp.concatenate([traces, next_block], 0))
    near_scale = jnp.concatenate([scale, next_scale], 0)
    pair_scale = far_scale[:, None] * near_scale[None, :] * time_scale
    bins = jnp.concatenate([pair_bins[0], next_bins], 0).T
    part = None
    for k, chunk in enumerate(far_chunks):
        rows = slice(k * size, (k + 1) * size)
        part = chunk_stack(chunk, near, pair_scale[rows], bins[rows], part)
    pair_total = ROUNDS * chan_count * channels * channels // NB
    part = part.T * (1.0 / math.sqrt(pair_total))
    part = jnp.pad(part, ((0, 0), (0, -part.shape[1] % LANES)))
    return reduce_all(part).T[:LAGS][::-1]


def solution(mesh):
    in_specs = (P("chan", "seg"), P(None, "chan", None))
    out_specs = P(None, "chan")
    return jax.shard_map(local, mesh=mesh, in_specs=in_specs, out_specs=out_specs, check_vma=False)
```

```python
import functools
import math

import jax
import jax.numpy as jnp
from jax import lax
from jax.experimental import pallas as pl
from jax.experimental.pallas import tpu as pltpu
from jax.sharding import PartitionSpec as P

MAX_LAG = 32
NB = 256
ROUNDS = 2
LAGS = 2 * MAX_LAG + 1
EPSILON = 1e-06

FINE = 8
COARSE = MAX_LAG // FINE
LANES = 128
CHUNKS = 4
MESH = pl.DeviceIdType.MESH
CONTRACT = (((1,), (1,)), ((), ()))


def whole_kernel(
    n_chan, n_seg, group, total_time, factor,
    traces_ref, energy_ref, bins_ref, later_bins_ref, out_ref,
    near, next_block, next_bins, far, scale_rows, energies, mine, scales_in,
    fine, neg, pos, last, total, part, arrived, second, others,
    send_e, recv_e, send_s, recv_s, send_n, recv_n, send_f, recv_f, send_1, recv_1, send_2, recv_2,
):
    chan, seg = lax.axis_index("chan"), lax.axis_index("seg")
    channels, length = traces_ref.shape
    width = 2 * channels
    size = channels // CHUNKS
    half = n_chan // 2
    rows = out_ref.shape[0]
    chan_peers = [lax.rem(chan + k, n_chan) for k in range(1, n_chan)]
    seg_peers = [lax.rem(seg + k, n_seg) for k in range(1, n_seg)]
    one_back = lax.rem(chan + n_chan - 1, n_chan)
    half_back = lax.rem(chan + n_chan - half, n_chan)

    def remote(source, target, send, recv, chan_to, seg_to):
        return pltpu.make_async_remote_copy(
            src_ref=source,
            dst_ref=target,
            send_sem=send,
            recv_sem=recv,
            device_id=(chan_to, seg_to),
            device_id_type=MESH,
        )

    def segment_sum(own, received):
        for position in range(n_seg):
            slot = lax.rem(seg - position + 2 * n_seg - 1, n_seg)
            term = jnp.where(slot == n_seg - 1, own, received[jnp.minimum(slot, n_seg - 2)])
            sums = term if position == 0 else sums + term
        return sums

    def dot(left, right):
        return lax.dot_general(left, right, CONTRACT, preferred_element_type=jnp.float32)

    barrier = pltpu.get_barrier_semaphore()
    for peer in chan_peers:
        pl.semaphore_signal(barrier, inc=1, device_id=(peer, seg), device_id_type=MESH)
    for peer in seg_peers:
        pl.semaphore_signal(barrier, inc=1, device_id=(chan, peer), device_id_type=MESH)
    pl.semaphore_wait(barrier, n_chan + n_seg - 2)

    energy_copies = [
        remote(energy_ref, energies.at[k], send_e.at[k], recv_e.at[k], chan, peer) for k, peer in enumerate(seg_peers)
    ]
    next_copies = [
        remote(traces_ref, next_block, send_n.at[0], recv_n.at[0], one_back, seg),
        remote(later_bins_ref, next_bins, send_n.at[1], recv_n.at[1], one_back, seg),
    ]
    for copy in energy_copies + next_copies:
        copy.start()
    for copy in energy_copies:
        copy.wait()
    own_scale = lax.rsqrt(segment_sum(energy_ref[...], energies) / total_time + EPSILON)
    mine[...] = own_scale
    scale_copies = [
        remote(mine, scales_in.at[k], send_s.at[k], recv_s.at[k], peer, seg)
        for k, peer in enumerate((one_back, half_back))
    ]
    for copy in scale_copies:
        copy.start()

    def far_copy(k):
        start = pl.multiple_of(k * size, size)
        return remote(traces_ref.at[pl.ds(start, size)], far.at[k], send_f.at[k], recv_f.at[k], half_back, seg)

    for k in range(CHUNKS):
        far_copy(k).start()

    tile = 16
    margin = jnp.zeros((tile, LANES), jnp.float32)

    def spread(source, offset):
        @pl.loop(0, channels // tile)
        def _(g):
            start = pl.multiple_of(g * tile, tile)
            block = source[pl.ds(start, tile), :]
            wide = jnp.concatenate([block.astype(jnp.float32), margin], 1)
            for k in range(2 * COARSE):
                shift = (k - COARSE + 1) * FINE
                if shift:
                    moved = pltpu.roll(wide, -shift % (length + LANES), 1)[:, :length].astype(jnp.bfloat16)
                else:
                    moved = block
                near[pl.ds(pl.multiple_of(k * width + offset + start, tile), tile), :] = moved

    spread(traces_ref, 0)
    for copy in next_copies:
        copy.wait()
    spread(next_block, channels)
    for copy in scale_copies:
        copy.wait()
    far_scale = jnp.transpose(jnp.broadcast_to(scales_in[1][:1], (channels, channels))) * (1.0 / math.sqrt(total_time))
    scale_rows[:, :channels] = far_scale * jnp.broadcast_to(mine[:1], (channels, channels))
    scale_rows[:, channels:] = far_scale * jnp.broadcast_to(scales_in[0][:1], (channels, channels))

    bin_ids = lax.broadcasted_iota(jnp.int32, (NB, width), 0)
    total[...] = jnp.zeros_like(total)
    pair = 2
    blank = jnp.zeros((FINE, LANES), jnp.float32)

    @pl.loop(0, CHUNKS)
    def _(chunk):
        far_copy(chunk).wait_recv()

        @pl.loop(0, size // tile)
        def _(g):
            wide = far[chunk, pl.ds(pl.multiple_of(g * tile, tile), tile), :].astype(jnp.float32)
            for start in range(0, tile, pair):
                both = []
                for x in range(start, start + pair):
                    row = jnp.broadcast_to(wide[x : x + 1], (FINE, length))
                    both.append(jnp.concatenate([row, blank], 1))
                first = pl.multiple_of((g * tile + start) * FINE, pair * FINE)
                for side, base in ((0, LANES + length - FINE), (1, 0)):
                    turned = [pltpu.roll(row, base, 1, stride=1, stride_axis=0)[:, :length] for row in both]
                    fine[side, pl.ds(first, pair * FINE), :] = jnp.concatenate(turned, 0).astype(jnp.bfloat16)

        neg[...] = dot(fine[0], near[: COARSE * width])
        pos[...] = dot(fine[1], near[(COARSE - 1) * width : (2 * COARSE - 1) * width])
        last[...] = dot(far[chunk], near[(2 * COARSE - 1) * width :])

        @pl.loop(0, size // group)
        def _(g):
            base = pl.multiple_of(g * group, group)
            here = pl.ds(pl.multiple_of(chunk * size + base, group), group)
            scale = scale_rows[here, :]
            bins = jnp.concatenate([bins_ref[here, :], next_bins[here, :]], 1)
            top = last[pl.ds(base, group), :]
            for first in range(0, group, group // 2):
                scores, hots = [], []
                for x in range(first, first + group // 2):
                    lines = pl.ds(pl.multiple_of((base + x) * FINE, FINE), FINE)
                    weight = jnp.broadcast_to(scale[x : x + 1], (FINE, width))
                    pieces = []
                    for side in (neg, pos):
                        for k in range(COARSE):
                            pieces.append(side[lines, k * width : (k + 1) * width] * weight)
                    edge = jnp.broadcast_to(top[x : x + 1], (FINE, width)) * weight
                    pieces += [edge, edge]
                    scores.append(jnp.concatenate(pieces, 0).astype(jnp.bfloat16))
                    hit = jnp.broadcast_to(bins[x : x + 1], (NB, width)) == bin_ids
                    hots.append(jnp.where(hit, 1.0, 0.0).astype(jnp.bfloat16))
                total[...] += dot(jnp.concatenate(scores, 1), jnp.concatenate(hots, 1))

    filler = jnp.zeros((LANES - total.shape[0], NB), jnp.float32)
    part[...] = jnp.transpose(jnp.concatenate([total[...] * factor, filler], 0))

    first_copies = []
    for k, peer in enumerate(chan_peers):
        owned = pl.ds(pl.multiple_of(peer * rows, rows), rows)
        first_copies.append(remote(part.at[owned], arrived.at[k], send_1.at[k], recv_1.at[k], peer, seg))
    for copy in first_copies:
        copy.start()
    running = part[pl.ds(pl.multiple_of(chan * rows, rows), rows), :]
    for k, copy in enumerate(first_copies):
        copy.wait()
        running = running + arrived[k]
    second[...] = running
    second_copies = [
        remote(second, others.at[k], send_2.at[k], recv_2.at[k], chan, peer) for k, peer in enumerate(seg_peers)
    ]
    for copy in second_copies:
        copy.start()
    for copy in second_copies:
        copy.wait()
    out_ref[...] = segment_sum(second[...], others)
    for k in range(CHUNKS):
        far_copy(k).wait_send()


def local(traces, pair_bins):
    channels, length = traces.shape
    n_chan, n_seg = lax.axis_size("chan"), lax.axis_size("seg")
    total_time = length * n_seg
    pair_total = ROUNDS * n_chan * channels * channels // NB
    energy = jnp.sum(jnp.square(traces.astype(jnp.float32)), axis=1)
    energy = jnp.broadcast_to(energy[None], (8, channels))
    width, size, rows = 2 * channels, channels // CHUNKS, NB // n_chan
    lag_rows = 2 * MAX_LAG + 2 * FINE
    f32, bf16 = jnp.float32, jnp.bfloat16
    counts = (n_seg - 1, 2, 2, CHUNKS, n_chan - 1, n_seg - 1)
    out = pl.pallas_call(
        functools.partial(whole_kernel, n_chan, n_seg, 8, total_time, 1.0 / math.sqrt(pair_total)),
        out_shape=jax.ShapeDtypeStruct((rows, LANES), f32),
        in_specs=[pl.BlockSpec(memory_space=pltpu.VMEM)] * 4,
        out_specs=pl.BlockSpec(memory_space=pltpu.VMEM),
        scratch_shapes=[
            pltpu.VMEM((2 * COARSE * width, length), bf16),
            pltpu.VMEM((channels, length), bf16),
            pltpu.VMEM((channels, channels), jnp.int32),
            pltpu.VMEM((CHUNKS, size, length), bf16),
            pltpu.VMEM((channels, width), f32),
            pltpu.VMEM((n_seg - 1, 8, channels), f32),
            pltpu.VMEM((8, channels), f32),
            pltpu.VMEM((2, 8, channels), f32),
            pltpu.VMEM((2, size * FINE, length), bf16),
            pltpu.VMEM((size * FINE, COARSE * width), f32),
            pltpu.VMEM((size * FINE, COARSE * width), f32),
            pltpu.VMEM((size, width), f32),
            pltpu.VMEM((lag_rows, NB), f32),
            pltpu.VMEM((NB, LANES), f32),
            pltpu.VMEM((n_chan - 1, rows, LANES), f32),
            pltpu.VMEM((rows, LANES), f32),
            pltpu.VMEM((n_seg - 1, rows, LANES), f32),
        ]
        + [pltpu.SemaphoreType.DMA((count,)) for count in counts for _ in range(2)],
        compiler_params=pltpu.CompilerParams(
            collective_id=0, has_side_effects=True, vmem_limit_bytes=40 * 1024 * 1024
        ),
    )(traces, energy, pair_bins[0].T, pair_bins[1].T)
    return out.T[:LAGS][::-1]


def solution(mesh):
    in_specs = (P("chan", "seg"), P(None, "chan", None))
    out_specs = P(None, "chan")
    return jax.shard_map(local, mesh=mesh, in_specs=in_specs, out_specs=out_specs, check_vma=False)
```

```python
import functools
import math

import jax
import jax.numpy as jnp
from jax import lax
from jax.experimental import pallas as pl
from jax.experimental.pallas import tpu as pltpu
from jax.sharding import PartitionSpec as P

MAX_LAG = 32
NB = 256
ROUNDS = 2
LAGS = 2 * MAX_LAG + 1
EPSILON = 1e-06

FINE = 8
COARSE = MAX_LAG // FINE
LANES = 128
CHUNKS = 4
MESH = pl.DeviceIdType.MESH
CONTRACT = (((1,), (1,)), ((), ()))


def whole_kernel(
    n_chan, n_seg, group, total_time, factor,
    traces_ref, energy_ref, bins_ref, later_bins_ref, out_ref,
    near, next_block, next_bins, far, scale_rows, energies, mine, scales_in,
    fine, neg, pos, last, total, part, arrived, second, others,
    send_e, recv_e, send_s, recv_s, send_n, recv_n, send_f, recv_f, send_1, recv_1, send_2, recv_2,
):
    chan, seg = lax.axis_index("chan"), lax.axis_index("seg")
    channels, length = traces_ref.shape
    width = 2 * channels
    size = channels // CHUNKS
    half = n_chan // 2
    rows = out_ref.shape[0]
    chan_peers = [lax.rem(chan + k, n_chan) for k in range(1, n_chan)]
    seg_peers = [lax.rem(seg + k, n_seg) for k in range(1, n_seg)]
    one_back = lax.rem(chan + n_chan - 1, n_chan)
    half_back = lax.rem(chan + n_chan - half, n_chan)

    def remote(source, target, send, recv, chan_to, seg_to):
        return pltpu.make_async_remote_copy(
            src_ref=source,
            dst_ref=target,
            send_sem=send,
            recv_sem=recv,
            device_id=(chan_to, seg_to),
            device_id_type=MESH,
        )

    def segment_sum(own, received):
        for position in range(n_seg):
            slot = lax.rem(seg - position + 2 * n_seg - 1, n_seg)
            term = jnp.where(slot == n_seg - 1, own, received[jnp.minimum(slot, n_seg - 2)])
            sums = term if position == 0 else sums + term
        return sums

    def dot(left, right):
        return lax.dot_general(left, right, CONTRACT, preferred_element_type=jnp.float32)

    barrier = pltpu.get_barrier_semaphore()
    for peer in chan_peers:
        pl.semaphore_signal(barrier, inc=1, device_id=(peer, seg), device_id_type=MESH)
    for peer in seg_peers:
        pl.semaphore_signal(barrier, inc=1, device_id=(chan, peer), device_id_type=MESH)
    pl.semaphore_wait(barrier, n_chan + n_seg - 2)

    energy_copies = [
        remote(energy_ref, energies.at[k], send_e.at[k], recv_e.at[k], chan, peer) for k, peer in enumerate(seg_peers)
    ]
    next_copies = [
        remote(later_bins_ref, next_bins, send_n.at[1], recv_n.at[1], one_back, seg),
        remote(traces_ref, next_block, send_n.at[0], recv_n.at[0], one_back, seg),
    ]
    for copy in energy_copies:
        copy.start()
    for copy in energy_copies:
        copy.wait()
    own_scale = lax.rsqrt(segment_sum(energy_ref[...], energies) / total_time + EPSILON)
    mine[...] = own_scale
    scale_copies = [
        remote(mine, scales_in.at[k], send_s.at[k], recv_s.at[k], peer, seg)
        for k, peer in enumerate((one_back, half_back))
    ]
    for copy in scale_copies + next_copies:
        copy.start()

    def far_copy(k):
        start = pl.multiple_of(k * size, size)
        return remote(traces_ref.at[pl.ds(start, size)], far.at[k], send_f.at[k], recv_f.at[k], half_back, seg)

    for k in range(CHUNKS):
        far_copy(k).start()

    tile = 16
    margin = jnp.zeros((tile, LANES), jnp.float32)

    def spread(source, offset):
        @pl.loop(0, channels // tile)
        def _(g):
            start = pl.multiple_of(g * tile, tile)
            block = source[pl.ds(start, tile), :]
            wide = jnp.concatenate([block.astype(jnp.float32), margin], 1)
            for k in range(2 * COARSE):
                shift = (k - COARSE + 1) * FINE
                if shift:
                    moved = pltpu.roll(wide, -shift % (length + LANES), 1)[:, :length].astype(jnp.bfloat16)
                else:
                    moved = block
                near[pl.ds(pl.multiple_of(k * width + offset + start, tile), tile), :] = moved

    spread(traces_ref, 0)
    for copy in next_copies:
        copy.wait()
    spread(next_block, channels)
    for copy in scale_copies:
        copy.wait()
    far_scale = jnp.transpose(jnp.broadcast_to(scales_in[1][:1], (channels, channels))) * (1.0 / math.sqrt(total_time))
    scale_rows[:, :channels] = far_scale * jnp.broadcast_to(mine[:1], (channels, channels))
    scale_rows[:, channels:] = far_scale * jnp.broadcast_to(scales_in[0][:1], (channels, channels))

    bin_ids = lax.broadcasted_iota(jnp.int32, (NB, width), 0)
    total[...] = jnp.zeros_like(total)
    pair = 2
    blank = jnp.zeros((FINE, LANES), jnp.float32)

    @pl.loop(0, CHUNKS)
    def _(chunk):
        far_copy(chunk).wait_recv()

        @pl.loop(0, size // tile)
        def _(g):
            wide = far[chunk, pl.ds(pl.multiple_of(g * tile, tile), tile), :].astype(jnp.float32)
            for start in range(0, tile, pair):
                both = []
                for x in range(start, start + pair):
                    row = jnp.broadcast_to(wide[x : x + 1], (FINE, length))
                    both.append(jnp.concatenate([row, blank], 1))
                first = pl.multiple_of((g * tile + start) * FINE, pair * FINE)
                for side, base in ((0, LANES + length - FINE), (1, 0)):
                    turned = [pltpu.roll(row, base, 1, stride=1, stride_axis=0)[:, :length] for row in both]
                    fine[side, pl.ds(first, pair * FINE), :] = jnp.concatenate(turned, 0).astype(jnp.bfloat16)

        neg[...] = dot(fine[0], near[: COARSE * width])
        pos[...] = dot(fine[1], near[(COARSE - 1) * width : (2 * COARSE - 1) * width])
        last[...] = dot(far[chunk], near[(2 * COARSE - 1) * width :])

        @pl.loop(0, size // group)
        def _(g):
            base = pl.multiple_of(g * group, group)
            here = pl.ds(pl.multiple_of(chunk * size + base, group), group)
            scale = scale_rows[here, :]
            bins = jnp.concatenate([bins_ref[here, :], next_bins[here, :]], 1)
            top = last[pl.ds(base, group), :]
            for first in range(0, group, group // 2):
                scores, hots = [], []
                for x in range(first, first + group // 2):
                    lines = pl.ds(pl.multiple_of((base + x) * FINE, FINE), FINE)
                    weight = jnp.broadcast_to(scale[x : x + 1], (FINE, width))
                    pieces = []
                    for side in (neg, pos):
                        for k in range(COARSE):
                            pieces.append(side[lines, k * width : (k + 1) * width] * weight)
                    edge = jnp.broadcast_to(top[x : x + 1], (FINE, width)) * weight
                    pieces += [edge, edge]
                    scores.append(jnp.concatenate(pieces, 0).astype(jnp.bfloat16))
                    hit = jnp.broadcast_to(bins[x : x + 1], (NB, width)) == bin_ids
                    hots.append(jnp.where(hit, 1.0, 0.0).astype(jnp.bfloat16))
                total[...] += dot(jnp.concatenate(scores, 1), jnp.concatenate(hots, 1))

    filler = jnp.zeros((LANES - total.shape[0], NB), jnp.float32)
    part[...] = jnp.transpose(jnp.concatenate([total[...] * factor, filler], 0))

    first_copies = []
    for k, peer in enumerate(chan_peers):
        owned = pl.ds(pl.multiple_of(peer * rows, rows), rows)
        first_copies.append(remote(part.at[owned], arrived.at[k], send_1.at[k], recv_1.at[k], peer, seg))
    for copy in first_copies:
        copy.start()
    running = part[pl.ds(pl.multiple_of(chan * rows, rows), rows), :]
    for k, copy in enumerate(first_copies):
        copy.wait()
        running = running + arrived[k]
    second[...] = running
    second_copies = [
        remote(second, others.at[k], send_2.at[k], recv_2.at[k], chan, peer) for k, peer in enumerate(seg_peers)
    ]
    for copy in second_copies:
        copy.start()
    for copy in second_copies:
        copy.wait()
    out_ref[...] = segment_sum(second[...], others)
    for k in range(CHUNKS):
        far_copy(k).wait_send()


def local(traces, pair_bins):
    channels, length = traces.shape
    n_chan, n_seg = lax.axis_size("chan"), lax.axis_size("seg")
    total_time = length * n_seg
    pair_total = ROUNDS * n_chan * channels * channels // NB
    energy = jnp.sum(jnp.square(traces.astype(jnp.float32)), axis=1)
    energy = jnp.broadcast_to(energy[None], (8, channels))
    width, size, rows = 2 * channels, channels // CHUNKS, NB // n_chan
    lag_rows = 2 * MAX_LAG + 2 * FINE
    f32, bf16 = jnp.float32, jnp.bfloat16
    counts = (n_seg - 1, 2, 2, CHUNKS, n_chan - 1, n_seg - 1)
    out = pl.pallas_call(
        functools.partial(whole_kernel, n_chan, n_seg, 8, total_time, 1.0 / math.sqrt(pair_total)),
        out_shape=jax.ShapeDtypeStruct((rows, LANES), f32),
        in_specs=[pl.BlockSpec(memory_space=pltpu.VMEM)] * 4,
        out_specs=pl.BlockSpec(memory_space=pltpu.VMEM),
        scratch_shapes=[
            pltpu.VMEM((2 * COARSE * width, length), bf16),
            pltpu.VMEM((channels, length), bf16),
            pltpu.VMEM((channels, channels), jnp.int32),
            pltpu.VMEM((CHUNKS, size, length), bf16),
            pltpu.VMEM((channels, width), f32),
            pltpu.VMEM((n_seg - 1, 8, channels), f32),
            pltpu.VMEM((8, channels), f32),
            pltpu.VMEM((2, 8, channels), f32),
            pltpu.VMEM((2, size * FINE, length), bf16),
            pltpu.VMEM((size * FINE, COARSE * width), f32),
            pltpu.VMEM((size * FINE, COARSE * width), f32),
            pltpu.VMEM((size, width), f32),
            pltpu.VMEM((lag_rows, NB), f32),
            pltpu.VMEM((NB, LANES), f32),
            pltpu.VMEM((n_chan - 1, rows, LANES), f32),
            pltpu.VMEM((rows, LANES), f32),
            pltpu.VMEM((n_seg - 1, rows, LANES), f32),
        ]
        + [pltpu.SemaphoreType.DMA((count,)) for count in counts for _ in range(2)],
        compiler_params=pltpu.CompilerParams(
            collective_id=0, has_side_effects=True, vmem_limit_bytes=40 * 1024 * 1024
        ),
    )(traces, energy, pair_bins[0].T, pair_bins[1].T)
    return out.T[:LAGS][::-1]


def solution(mesh):
    in_specs = (P("chan", "seg"), P(None, "chan", None))
    out_specs = P(None, "chan")
    return jax.shard_map(local, mesh=mesh, in_specs=in_specs, out_specs=out_specs, check_vma=False)
```

```python
import functools
import math

import jax
import jax.numpy as jnp
from jax import lax
from jax.experimental import pallas as pl
from jax.experimental.pallas import tpu as pltpu
from jax.sharding import PartitionSpec as P


MAX_LAG = 32
NB = 256
ROUNDS = 2
LAGS = 2 * MAX_LAG + 1
EPSILON = 1e-06

FINE = 8
COARSE = MAX_LAG // FINE
LANES = 128
CHUNKS = 4
MESH = pl.DeviceIdType.MESH
CONTRACT = (((1,), (1,)), ((), ()))


def from_behind(block, axis, distance):
    devices = range(lax.axis_size(axis))
    route = [((i - distance) % len(devices), i) for i in devices]
    return lax.ppermute(block, axis, route)


def coarse_shifts(block):
    length = block.shape[1]
    padded = jnp.pad(block, ((0, 0), (MAX_LAG, MAX_LAG)))
    starts = range(FINE, 2 * MAX_LAG + 1, FINE)
    return jnp.concatenate([lax.slice_in_dim(padded, start, start + length, axis=1) for start in starts], 0)


def stack_kernel(group, first, far_ref, near_ref, scale_ref, bins_ref, prior_ref, out_ref, fine, neg, pos, last):
    channels, length = far_ref.shape
    width = near_ref.shape[0] // (2 * COARSE)

    def dot(left, right):
        return lax.dot_general(left, right, CONTRACT, preferred_element_type=jnp.float32)

    pair = 2
    tile = pair * FINE
    blank = jnp.zeros((FINE, LANES), jnp.float32)
    for block in range(channels // tile):
        wide = far_ref[block * tile : (block + 1) * tile, :].astype(jnp.float32)
        for start in range(0, tile, pair):
            both = []
            for x in range(start, start + pair):
                row = jnp.broadcast_to(wide[x : x + 1], (FINE, length))
                both.append(jnp.concatenate([row, blank], 1))
            rows = slice((block * tile + start) * FINE, (block * tile + start + pair) * FINE)
            for side, base in ((0, LANES + length - FINE), (1, 0)):
                turned = [pltpu.roll(row, base, 1, stride=1, stride_axis=0)[:, :length] for row in both]
                fine[side, rows, :] = jnp.concatenate(turned, 0).astype(jnp.bfloat16)

    neg[...] = dot(fine[0], near_ref[: COARSE * width])
    pos[...] = dot(fine[1], near_ref[(COARSE - 1) * width : (2 * COARSE - 1) * width])
    last[...] = dot(far_ref[...], near_ref[(2 * COARSE - 1) * width :])

    bin_ids = lax.broadcasted_iota(jnp.int32, (NB, width), 0)
    out_ref[...] = jnp.zeros_like(out_ref) if first else prior_ref[...]

    @pl.loop(0, channels // group)
    def _(g):
        base = pl.multiple_of(g * group, group)
        scale = scale_ref[pl.ds(base, group), :]
        bins = bins_ref[pl.ds(base, group), :]
        top = last[pl.ds(base, group), :]
        for half in range(0, group, group // 2):
            scores, hots = [], []
            for x in range(half, half + group // 2):
                rows = pl.ds(pl.multiple_of((base + x) * FINE, FINE), FINE)
                factor = jnp.broadcast_to(scale[x : x + 1], (FINE, width))
                pieces = []
                for side in (neg, pos):
                    for k in range(COARSE):
                        pieces.append(side[rows, k * width : (k + 1) * width] * factor)
                edge = jnp.broadcast_to(top[x : x + 1], (FINE, width)) * factor
                pieces += [edge, edge]
                scores.append(jnp.concatenate(pieces, 0).astype(jnp.bfloat16))
                hit = jnp.broadcast_to(bins[x : x + 1], (NB, width)) == bin_ids
                hots.append(jnp.where(hit, 1.0, 0.0).astype(jnp.bfloat16))
            out_ref[...] += dot(jnp.concatenate(scores, 1), jnp.concatenate(hots, 1))


def chunk_stack(far, near, scale, bins, prior):
    channels, length = far.shape
    width = near.shape[0] // (2 * COARSE)
    lag_rows = 2 * MAX_LAG + 2 * FINE
    first = prior is None
    if first:
        prior = jnp.zeros((8, LANES), jnp.float32)
    return pl.pallas_call(
        functools.partial(stack_kernel, 8, first),
        out_shape=jax.ShapeDtypeStruct((lag_rows, NB), jnp.float32),
        in_specs=[pl.BlockSpec(memory_space=pltpu.VMEM)] * 5,
        out_specs=pl.BlockSpec(memory_space=pltpu.VMEM),
        scratch_shapes=[
            pltpu.VMEM((2, channels * FINE, length), jnp.bfloat16),
            pltpu.VMEM((channels * FINE, COARSE * width), jnp.float32),
            pltpu.VMEM((channels * FINE, COARSE * width), jnp.float32),
            pltpu.VMEM((channels, width), jnp.float32),
        ],
        compiler_params=pltpu.CompilerParams(vmem_limit_bytes=32 * 1024 * 1024),
        cost_estimate=pl.CostEstimate(
            flops=2 * LAGS * channels * width * length, bytes_accessed=near.size * 2, transcendentals=0
        ),
    )(far, near, scale, bins, prior)


def reduce_kernel(n_chan, n_seg, part_ref, out_ref, arrived, mine, others, send1, recv1, send2, recv2):
    chan, seg = lax.axis_index("chan"), lax.axis_index("seg")
    rows = out_ref.shape[0]
    chan_peers = [lax.rem(chan + k, n_chan) for k in range(1, n_chan)]
    seg_peers = [lax.rem(seg + k, n_seg) for k in range(1, n_seg)]
    barrier = pltpu.get_barrier_semaphore()
    for peer in chan_peers:
        pl.semaphore_signal(barrier, inc=1, device_id=(peer, seg), device_id_type=MESH)
    for peer in seg_peers:
        pl.semaphore_signal(barrier, inc=1, device_id=(chan, peer), device_id_type=MESH)
    pl.semaphore_wait(barrier, n_chan + n_seg - 2)

    first = []
    for k, peer in enumerate(chan_peers):
        copy = pltpu.make_async_remote_copy(
            src_ref=part_ref.at[pl.ds(pl.multiple_of(peer * rows, rows), rows)],
            dst_ref=arrived.at[k],
            send_sem=send1.at[k],
            recv_sem=recv1.at[k],
            device_id=(peer, seg),
            device_id_type=MESH,
        )
        copy.start()
        first.append(copy)
    running = part_ref[pl.ds(pl.multiple_of(chan * rows, rows), rows), :]
    for k, copy in enumerate(first):
        copy.wait()
        running = running + arrived[k]
    mine[...] = running
    second = []
    for k, peer in enumerate(seg_peers):
        copy = pltpu.make_async_remote_copy(
            src_ref=mine,
            dst_ref=others.at[k],
            send_sem=send2.at[k],
            recv_sem=recv2.at[k],
            device_id=(chan, peer),
            device_id_type=MESH,
        )
        copy.start()
        second.append(copy)
    for copy in second:
        copy.wait()
    for position in range(n_seg):
        slot = lax.rem(seg - position + n_seg - 1 + n_seg, n_seg)
        term = jnp.where(slot == n_seg - 1, running, others[jnp.minimum(slot, n_seg - 2)])
        sums = term if position == 0 else sums + term
    out_ref[...] = sums


def reduce_all(part):
    n_chan, n_seg = lax.axis_size("chan"), lax.axis_size("seg")
    rows = part.shape[0] // n_chan
    block = (rows, part.shape[1])
    return pl.pallas_call(
        functools.partial(reduce_kernel, n_chan, n_seg),
        out_shape=jax.ShapeDtypeStruct(block, jnp.float32),
        in_specs=[pl.BlockSpec(memory_space=pltpu.VMEM)],
        out_specs=pl.BlockSpec(memory_space=pltpu.VMEM),
        scratch_shapes=[
            pltpu.VMEM((n_chan - 1,) + block, jnp.float32),
            pltpu.VMEM(block, jnp.float32),
            pltpu.VMEM((n_seg - 1,) + block, jnp.float32),
            pltpu.SemaphoreType.DMA((n_chan - 1,)),
            pltpu.SemaphoreType.DMA((n_chan - 1,)),
            pltpu.SemaphoreType.DMA((n_seg - 1,)),
            pltpu.SemaphoreType.DMA((n_seg - 1,)),
        ],
        compiler_params=pltpu.CompilerParams(
            collective_id=0, has_side_effects=True, vmem_limit_bytes=16 * 1024 * 1024
        ),
    )(part)


def scales_kernel(n_chan, n_seg, half, total_time, energy_ref, out_ref, mine, arrived, send1, recv1, send2, recv2):
    chan, seg = lax.axis_index("chan"), lax.axis_index("seg")
    seg_peers = [lax.rem(seg + k, n_seg) for k in range(1, n_seg)]
    barrier = pltpu.get_barrier_semaphore()
    for peer in seg_peers:
        pl.semaphore_signal(barrier, inc=1, device_id=(chan, peer), device_id_type=MESH)
    for distance in (1, half):
        giver = lax.rem(chan + distance, n_chan)
        pl.semaphore_signal(barrier, inc=1, device_id=(giver, seg), device_id_type=MESH)
    pl.semaphore_wait(barrier, n_seg + 1)

    copies = []
    for k, peer in enumerate(seg_peers):
        copy = pltpu.make_async_remote_copy(
            src_ref=energy_ref,
            dst_ref=arrived.at[k],
            send_sem=send1.at[k],
            recv_sem=recv1.at[k],
            device_id=(chan, peer),
            device_id_type=MESH,
        )
        copy.start()
        copies.append(copy)
    for copy in copies:
        copy.wait()
    for position in range(n_seg):
        slot = lax.rem(seg - position + 2 * n_seg - 1, n_seg)
        term = jnp.where(slot == n_seg - 1, energy_ref[...], arrived[jnp.minimum(slot, n_seg - 2)])
        total = term if position == 0 else total + term
    scale = lax.rsqrt(total / total_time + EPSILON)
    mine[...] = scale
    out_ref[0] = scale
    copies = []
    for k, distance in enumerate((1, half)):
        copy = pltpu.make_async_remote_copy(
            src_ref=mine,
            dst_ref=arrived.at[n_seg - 1 + k],
            send_sem=send2.at[k],
            recv_sem=recv2.at[k],
            device_id=(lax.rem(chan + n_chan - distance, n_chan), seg),
            device_id_type=MESH,
        )
        copy.start()
        copies.append(copy)
    for k, copy in enumerate(copies):
        copy.wait()
        out_ref[1 + k] = arrived[n_seg - 1 + k]


def scales_of(energy, half, total_time):
    n_chan, n_seg = lax.axis_size("chan"), lax.axis_size("seg")
    block = (8, energy.shape[0])
    rows = jnp.broadcast_to(energy[None], block)
    out = pl.pallas_call(
        functools.partial(scales_kernel, n_chan, n_seg, half, total_time),
        out_shape=jax.ShapeDtypeStruct((3,) + block, jnp.float32),
        in_specs=[pl.BlockSpec(memory_space=pltpu.VMEM)],
        out_specs=pl.BlockSpec(memory_space=pltpu.VMEM),
        scratch_shapes=[
            pltpu.VMEM(block, jnp.float32),
            pltpu.VMEM((n_seg + 1,) + block, jnp.float32),
            pltpu.SemaphoreType.DMA((n_seg - 1,)),
            pltpu.SemaphoreType.DMA((n_seg - 1,)),
            pltpu.SemaphoreType.DMA((2,)),
            pltpu.SemaphoreType.DMA((2,)),
        ],
        compiler_params=pltpu.CompilerParams(
            collective_id=1, has_side_effects=True, vmem_limit_bytes=4 * 1024 * 1024
        ),
    )(rows)
    return out[0, 0], out[1, 0], out[2, 0]


def local(traces, pair_bins):
    channels, seg_length = traces.shape
    chan_count = lax.axis_size("chan")
    seg_count = lax.axis_size("seg")
    total_time = seg_length * seg_count
    time_scale = 1.0 / math.sqrt(total_time)
    half_loop = chan_count // 2
    next_bins = from_behind(pair_bins[1], "chan", -1)
    energy = jnp.sum(jnp.square(traces.astype(jnp.float32)), axis=1)
    scale, next_scale, far_scale = scales_of(energy, half_loop, total_time)
    traces, scale, next_scale, far_scale = lax.optimization_barrier((traces, scale, next_scale, far_scale))
    next_block = from_behind(traces, "chan", -1)
    size = channels // CHUNKS
    far_chunks = []
    for k in range(CHUNKS):
        far_chunks.append(from_behind(traces[k * size : (k + 1) * size], "chan", -half_loop))
    near = coarse_shifts(jnp.concatenate([traces, next_block], 0))
    near_scale = jnp.concatenate([scale, next_scale], 0)
    pair_scale = far_scale[:, None] * near_scale[None, :] * time_scale
    bins = jnp.concatenate([pair_bins[0], next_bins], 0).T
    part = None
    for k, chunk in enumerate(far_chunks):
        rows = slice(k * size, (k + 1) * size)
        part = chunk_stack(chunk, near, pair_scale[rows], bins[rows], part)
    pair_total = ROUNDS * chan_count * channels * channels // NB
    part = part.T * (1.0 / math.sqrt(pair_total))
    part = jnp.pad(part, ((0, 0), (0, -part.shape[1] % LANES)))
    return reduce_all(part).T[:LAGS][::-1]


def solution(mesh):
    in_specs = (P("chan", "seg"), P(None, "chan", None))
    out_specs = P(None, "chan")

    return jax.shard_map(local, mesh=mesh, in_specs=in_specs, out_specs=out_specs, check_vma=False)
```
